32 devices in a mesh: wave: 4 (over y, x), event: 8 (over z, core).
Axes of the slice: x: 2, y: 2, z: 4, core: 2. Of those that a mesh axis runs over, the one named last changes fastest.
Arguments:
- latent: bfloat16 [8, 512, 2048], P(None, 'wave', 'event'), may hold values from -6 to 6
- basis: bfloat16 [262144, 512], P('event', 'wave'), may hold values from -0.29882812 to 0.29882812
- event_bin: int32 [8, 32768], P('event'), may hold values from 0 to 255, never falling along the last dimension, each value on 1 to 512 neighbouring positions
- length: float32 [512, 2048], P('wave', 'event'), may hold values from 0.01 to 0.08
- amplitude_scale: float32 [512, 2048], P('wave', 'event'), may hold values from 0.3 to 1
- yield_norm: float32 [512, 2048], P('wave', 'event'), may hold values from 0.5 to 2
- bin_coords: float32 [2, 2048], replicated, may hold values from 0 to 1
Outputs:
- grad_latent: float32 [8, 512, 2048], P(None, 'wave', 'event')
The draws below stay inside these ranges and needn't reach their ends.
Inputs may be any that keep to these rules, and one draw needn't show every extreme that they name: `event_bin`: along each block's events, bin numbers never fall and every one of the block's bins holds at least one event.
All inputs are finite; a program needn't handle non-finite values.
Results may differ from the reference program's by a relative error of at most 0.0024.
Values may be sent and summed in bfloat16 or wider, within the bound.
A program may use at most 256 MiB of HBM per device.

```python
import math
import jax
import jax.numpy as jnp
import numpy as np
from jax import lax

B = 2048
W = 512
S = 8
EV_DEV = 32768
NBLOCKS = 8
EVENTS = 262144
N_EVENT = 8


def block_scale(own_key, shape, split, least, largest):
    def one(position, blocks):
        steps = jax.random.uniform(jax.random.fold_in(jax.random.fold_in(own_key, 6), position), (blocks,), jnp.float32, least / len(split), largest / len(split))
        return jnp.repeat(jnp.exp(steps), shape[position] // blocks).reshape((-1,) + (1,) * (len(shape) - position - 1))

    gain = one(*split[0])
    for cut in split[1:]:
        gain = gain * one(*cut)
    return gain


def length_profile(amount, total, most, lean):
    portions = [(1 << 20) // math.isqrt(grade ** lean) + 1 for grade in range(2, amount + 1)]
    spare, counts = total - most - (amount - 1), [1] * (amount - 1)
    while spare > 0:
        candidates = [i for i in range(amount - 1) if counts[i] < most]
        pool, budget = sum([portions[i] for i in candidates]), spare
        for i in candidates:
            addition = min(most - counts[i], max(1, budget * portions[i] // pool), spare)
            counts[i] = counts[i] + addition
            spare = spare - addition
    return np.array([most] + counts)


def uneven(stream_key, amount, total, bound, skew):
    if amount == 2:
        one = jax.random.randint(stream_key, (), max(1, total - bound), min(bound, total - 1) + 1)
        return jnp.stack([one, total - one])
    tallies = jnp.asarray(length_profile(amount, total, bound, skew), jnp.int32)
    couples = (amount - 1) // 2
    source_of, receiver = tallies[1:1 + 2 * couples:2], tallies[2:2 + 2 * couples:2]
    slack = jnp.minimum(source_of - 1, bound - receiver)
    passed = jax.random.randint(jax.random.fold_in(stream_key, 1), (couples,), 0, 1 << 20) % (slack + 1)
    tallies = tallies.at[1:1 + 2 * couples:2].set(source_of - passed).at[2:2 + 2 * couples:2].set(receiver + passed)
    return tallies[jax.random.permutation(jax.random.fold_in(stream_key, 2), amount)]


def gaussian(rng, dims, width, reach, cuts=(), held_as=jnp.bfloat16):
    factor_of = block_scale(rng, dims, cuts, -0.22, 0.18) if cuts else 1.0
    drawn = jax.random.normal(rng, dims, jnp.float32) * width * factor_of
    return jnp.minimum(jnp.maximum(drawn, -reach), reach).astype(held_as)


def setup_inputs(seed: int = 0) -> dict:
    key_of = jax.random.split(jax.random.key(seed), 8)
    return {
        "latent": gaussian(key_of[0], (S, W, B), 1.0, 6.0, ((1, 4), (2, 8))),
        "basis": gaussian(key_of[1], (EVENTS, W), 0.05, 0.29882812, ((0, 8), (1, 4))),
        "event_bin": jax.vmap(lambda own: jnp.searchsorted(jnp.cumsum(uneven(own, B // N_EVENT, EV_DEV, min(4 * EV_DEV // (B // N_EVENT), EV_DEV - B // N_EVENT + 1), 2)), jnp.arange(EV_DEV), side="right"))(jax.random.split(key_of[2], NBLOCKS)).reshape((NBLOCKS, EV_DEV)).astype(jnp.int32),
        "length": jnp.clip(jnp.exp(math.log(0.08) - 2.0794415 * jax.random.uniform(key_of[3], (W, B), jnp.float32) ** block_scale(key_of[3], (W, B), ((0, 4), (1, 8)), -0.2, 0.2)), 0.01, 0.08),
        "amplitude_scale": jnp.clip(jnp.exp(math.log(1.0) - 1.2039728 * jax.random.uniform(key_of[4], (W, B), jnp.float32) ** block_scale(key_of[4], (W, B), ((0, 4), (1, 8)), -0.2, 0.2)), 0.3, 1.0),
        "yield_norm": jnp.clip(jnp.exp(math.log(2.0) - 1.3862944 * jax.random.uniform(key_of[5], (W, B), jnp.float32) ** block_scale(key_of[5], (W, B), ((0, 4), (1, 8)), -0.2, 0.2)), 0.5, 2.0),
        "bin_coords": jnp.clip(jax.random.uniform(key_of[6], (2, B), jnp.float32, 0.0, 1.0), 0.0, 1.0),
    }


def gibbs(rows_xy, cols_xy, len_rows, amp_rows, len_cols, amp_cols):
    diff_x = rows_xy[0][:, None] - cols_xy[0][None, :]
    diff_y = rows_xy[1][:, None] - cols_xy[1][None, :]
    dist = diff_x * diff_x + diff_y * diff_y
    left = len_rows[:, :, None]
    right = len_cols[:, None, :]
    spread = left * left + right * right
    return amp_rows[:, :, None] * amp_cols[:, None, :] * jnp.sqrt(2.0 * (left * right) / spread) * jnp.exp(-dist / spread)

def reference(latent, basis, event_bin, length, amplitude_scale, yield_norm, bin_coords):
    rows = B // N_EVENT

    def wave_kernel(w_index):
        len_wave = length[w_index][None]
        amp_wave = amplitude_scale[w_index][None]
        return gibbs(bin_coords, bin_coords, len_wave, amp_wave, len_wave, amp_wave)[0].astype(jnp.bfloat16)

    def forward_wave(w_index):
        kern = wave_kernel(w_index)
        return jnp.dot(kern, latent[:, w_index, :].T, preferred_element_type=jnp.float32)
    amps = lax.map(forward_wave, jnp.arange(W, dtype=jnp.int32))
    amplitude = jnp.transpose(amps, (2, 0, 1)).astype(jnp.bfloat16)
    basis_blocks = basis.reshape(NBLOCKS, EV_DEV, W)

    def block_sums(pieces):
        blk, psi, seg = pieces
        local = lax.dynamic_slice_in_dim(amplitude, (blk * rows).astype(jnp.int32), rows, 2).astype(jnp.float32)
        picked = jnp.transpose(local, (2, 0, 1))[seg]
        psi_wide = psi.astype(jnp.float32)
        field = lax.optimization_barrier(jnp.sum(picked * psi_wide[:, None, :], axis=2))
        weight = -2.0 * field / (1.0 + field * field) / S
        terms = (weight[:, :, None] * psi_wide[:, None, :]).astype(jnp.bfloat16)
        terms = lax.optimization_barrier(terms).astype(jnp.float32)
        return jax.ops.segment_sum(terms, seg, num_segments=rows)
    sums = lax.map(block_sums, (jnp.arange(NBLOCKS, dtype=jnp.int32), basis_blocks, event_bin))
    sums = sums.reshape(B, S, W)
    yield_term = 2.0 / S * amplitude.astype(jnp.float32) * yield_norm[None]
    bin_grad = (sums + jnp.transpose(yield_term, (2, 0, 1))).astype(jnp.bfloat16)

    def backward_wave(w_index):
        kern = wave_kernel(w_index)
        return jnp.dot(kern, bin_grad[:, :, w_index], preferred_element_type=jnp.float32)
    grads = lax.map(backward_wave, jnp.arange(W, dtype=jnp.int32))
    return jnp.transpose(grads, (2, 0, 1)) + latent.astype(jnp.float32)
```

```python
import functools
import math

import jax
import jax.numpy as jnp
from jax import lax
from jax.experimental import pallas as pl
from jax.experimental.pallas import tpu as pltpu
from jax.sharding import PartitionSpec as P

TILE = 256
LANES = 128
CHUNK = 512
GROUP = 16
NN = (((1,), (0,)), ((), ()))
NT = (((1,), (1,)), ((), ()))


def dot(a, b, dims):
    return lax.dot_general(a, b, dims, preferred_element_type=jnp.float32)


def spread_rows(dst, read, total):
    for k in range(total // LANES):
        row = read(k * LANES)
        dst[pl.ds(k * LANES, LANES), :] = jnp.broadcast_to(row, (LANES, LANES)).T


def gather_pieces(dst, src, pieces, width):
    for k in range(pieces):
        block, lane = (k * width) // TILE, (k * width) % TILE
        dst[block, :, lane : lane + width] = src(k)


def wide(column):
    return jnp.concatenate([column] * (TILE // LANES), axis=1)


def forward_kernel(pieces, width, coords, profile, latent, kern, amp, dist, col_l, col_g, prof, vec, acc):
    total = pieces * width
    blocks = total // TILE
    step = 64

    @pl.when(pl.program_id(0) == 0)
    def _():
        spread_rows(col_l, lambda k: coords[0:1, k : k + LANES], total)
        spread_rows(col_g, lambda k: coords[1:2, k : k + LANES], total)

        def over_i(i, t0):
            def over_j(j, t):
                col = pl.ds(pl.multiple_of(j * TILE, TILE), TILE)
                x_c, y_c = coords[0:1, col], coords[1:2, col]
                for r in range(0, TILE, step):
                    row = pl.ds(pl.multiple_of(i * TILE + r, step), step)
                    dx = wide(col_l[row, :]) - x_c
                    dy = wide(col_g[row, :]) - y_c
                    dist[t, r : r + step, :] = (dx * dx + dy * dy) * (-math.log2(math.e))
                return t + 1

            return lax.fori_loop(i, blocks, over_j, t0)

        lax.fori_loop(0, blocks, over_i, 0)

    gather_pieces(prof, lambda k: profile[k, 0], pieces, width)
    gather_pieces(vec, lambda k: latent[k, 0], pieces, width)
    per = TILE // LANES
    spread_rows(col_l, lambda k: prof[k // TILE, 0:1, k % TILE : k % TILE + LANES], total)
    spread_rows(col_g, lambda k: prof[k // TILE, 1:2, k % TILE : k % TILE + LANES], total)
    acc[...] = jnp.zeros_like(acc)

    def build(i, j, t):
        l_c, g_c = prof[j, 0:1, :], prof[j, 1:2, :]
        for r in range(0, TILE, step):
            row = pl.ds(pl.multiple_of(i * TILE + r, step), step)
            root = lax.rsqrt(wide(col_l[row, :]) + l_c)
            power = jnp.exp2(dist[t, r : r + step, :] * (root * root))
            scale = wide(col_g[row, :]) * g_c
            kern[0, t, r : r + step, :] = (scale * root * power).astype(jnp.bfloat16)

    def over_i(i, t0):
        build(i, i, t0)
        acc[i] += dot(vec[i], kern[0, t0], NN)

        def over_j(j, t):
            build(i, j, t)
            tile = kern[0, t]
            acc[j] += dot(vec[i], tile, NN)
            acc[i] += dot(vec[j], tile, NT)
            return t + 1

        return lax.fori_loop(i + 1, blocks, over_j, t0 + 1)

    lax.fori_loop(0, blocks, over_i, 0)
    for k in range(pieces):
        block, lane = (k * width) // TILE, (k * width) % TILE
        amp[k, 0] = acc[block, :, lane : lane + width].astype(amp.dtype)


def backward_kernel(pieces, width, kern, grad, out, vec, acc):
    total = pieces * width
    blocks = total // TILE
    gather_pieces(vec, lambda k: grad[k, 0], pieces, width)
    acc[...] = jnp.zeros_like(acc)

    def over_i(i, t0):
        acc[i] += dot(vec[i], kern[0, t0], NN)

        def over_j(j, t):
            tile = kern[0, t]
            acc[j] += dot(vec[i], tile, NN)
            acc[i] += dot(vec[j], tile, NT)
            return t + 1

        return lax.fori_loop(i + 1, blocks, over_j, t0 + 1)

    lax.fori_loop(0, blocks, over_i, 0)
    for k in range(pieces):
        block, lane = (k * width) // TILE, (k * width) % TILE
        out[k, 0] = acc[block, :, lane : lane + width].astype(out.dtype)


def field_kernel(samples, inner, first, last, rows, basis, label, field):
    span = GROUP * samples
    base = pl.program_id(0) * inner

    def one(c, _):
        at = pl.ds(pl.multiple_of(c * CHUNK, CHUNK), CHUNK)
        psi = basis[at, :]
        seg = jnp.broadcast_to(label[:, at], (samples, CHUNK))

        def over_g(g, total):
            part = rows[pl.ds(pl.multiple_of(g * span, span), span), :]
            full = dot(part, psi, NT)
            own = seg - g * GROUP
            for b in range(GROUP):
                total = total + jnp.where(own == b, full[b * samples : (b + 1) * samples, :], 0.0)
            return total

        start = jnp.zeros((samples, CHUNK), jnp.float32)
        field[:, at] = lax.fori_loop(first[base + c], last[base + c] + 1, over_g, start)
        return 0

    lax.fori_loop(0, inner, one, 0)


def sums_kernel(samples, inner, first, last, field, basis, label, sums):
    span = GROUP * samples
    base = pl.program_id(0) * inner

    @pl.when(pl.program_id(0) == 0)
    def _():
        sums[...] = jnp.zeros_like(sums)

    def one(c, _):
        at = pl.ds(pl.multiple_of(c * CHUNK, CHUNK), CHUNK)
        psi = basis[at, :]
        seg = jnp.broadcast_to(label[:, at], (samples, CHUNK))
        value = field[:, at]
        weight = -2.0 * value / (1.0 + value * value) / samples

        def over_g(g, _):
            own = seg - g * GROUP
            full = jnp.concatenate([jnp.where(own == b, weight, 0.0) for b in range(GROUP)], axis=0)
            high = full.astype(jnp.bfloat16)
            low = (full - high.astype(jnp.float32)).astype(jnp.bfloat16)
            at_g = pl.ds(pl.multiple_of(g * span, span), span)
            sums[at_g, :] += dot(high, psi, NN) + dot(low, psi, NN)
            return 0

        return lax.fori_loop(first[base + c], last[base + c] + 1, over_g, 0)

    lax.fori_loop(0, inner, one, 0)


def params(limit=60 << 20):
    return pltpu.CompilerParams(dimension_semantics=("arbitrary",), vmem_limit_bytes=limit)


def shards(count, latent, basis, event_bin, length, amplitude_scale, yield_norm, bin_coords):
    samples, waves, width = latent.shape
    total = bin_coords.shape[1]
    own = waves // count
    blocks = total // TILE
    tiles = blocks * (blocks + 1) // 2
    f32, bf16 = jnp.float32, jnp.bfloat16

    def exchange(values):
        return lax.all_to_all(values, "event", 0, 0)

    profile = jnp.stack(
        [length * length, amplitude_scale * jnp.sqrt(math.sqrt(2.0) * length)], axis=1
    ).reshape(count, own, 2, width)
    profile = exchange(profile)
    draws = exchange(jnp.transpose(latent, (1, 0, 2)).reshape(count, own, samples, width))

    piece = pl.BlockSpec((count, 1, samples, width), lambda w: (0, w, 0, 0))
    kern_spec = pl.BlockSpec((1, tiles, TILE, TILE), lambda w: (w, 0, 0, 0))
    kern, amp = pl.pallas_call(
        functools.partial(forward_kernel, count, width),
        out_shape=(
            jax.ShapeDtypeStruct((own, tiles, TILE, TILE), bf16),
            jax.ShapeDtypeStruct((count, own, samples, width), bf16),
        ),
        grid=(own,),
        in_specs=[
            pl.BlockSpec((2, total), lambda w: (0, 0)),
            pl.BlockSpec((count, 1, 2, width), lambda w: (0, w, 0, 0)),
            piece,
        ],
        out_specs=(kern_spec, piece),
        scratch_shapes=[
            pltpu.VMEM((tiles, TILE, TILE), f32),
            pltpu.VMEM((total, LANES), f32),
            pltpu.VMEM((total, LANES), f32),
            pltpu.VMEM((blocks, 2, TILE), f32),
            pltpu.VMEM((blocks, samples, TILE), bf16),
            pltpu.VMEM((blocks, samples, TILE), f32),
        ],
        compiler_params=params(),
        name="kern_forward",
    )(bin_coords, profile, draws)

    amp = exchange(amp).reshape(waves, samples, width)
    amp_rows = jnp.transpose(amp, (2, 1, 0)).reshape(width * samples, waves)

    events = basis.shape[0]
    block = min(events, 4096)
    inner = block // CHUNK
    grouped = event_bin.reshape(events // CHUNK, CHUNK) // GROUP
    first, last = grouped[:, 0], grouped[:, -1]
    basis_spec = pl.BlockSpec((block, waves), lambda e, *_: (e, 0))
    label_spec = pl.BlockSpec((1, block), lambda e, *_: (0, e))
    field_spec = pl.BlockSpec((samples, block), lambda e, *_: (0, e))
    rows_spec = pl.BlockSpec((width * samples, waves), lambda e, *_: (0, 0))
    field = pl.pallas_call(
        functools.partial(field_kernel, samples, inner),
        out_shape=jax.ShapeDtypeStruct((samples, events), f32),
        grid_spec=pltpu.PrefetchScalarGridSpec(
            num_scalar_prefetch=2,
            grid=(events // block,),
            in_specs=[rows_spec, basis_spec, label_spec],
            out_specs=field_spec,
        ),
        compiler_params=params(),
        name="event_field",
    )(first, last, amp_rows, basis, event_bin)
    field = lax.psum(field, "wave")
    sums = pl.pallas_call(
        functools.partial(sums_kernel, samples, inner),
        out_shape=jax.ShapeDtypeStruct((width * samples, waves), f32),
        grid_spec=pltpu.PrefetchScalarGridSpec(
            num_scalar_prefetch=2,
            grid=(events // block,),
            in_specs=[field_spec, basis_spec, label_spec],
            out_specs=rows_spec,
        ),
        compiler_params=params(),
        name="event_sums",
    )(first, last, field, basis, event_bin)

    sums = jnp.transpose(sums.reshape(width, samples, waves), (2, 1, 0))
    grad = (sums + 2.0 / samples * amp.astype(f32) * yield_norm[:, None, :]).astype(bf16)
    grad = exchange(grad.reshape(count, own, samples, width))
    pulled = pl.pallas_call(
        functools.partial(backward_kernel, count, width),
        out_shape=jax.ShapeDtypeStruct((count, own, samples, width), f32),
        grid=(own,),
        in_specs=[kern_spec, piece],
        out_specs=piece,
        scratch_shapes=[
            pltpu.VMEM((blocks, samples, TILE), bf16),
            pltpu.VMEM((blocks, samples, TILE), f32),
        ],
        compiler_params=params(),
        name="kern_backward",
    )(kern, grad)
    pulled = exchange(pulled).reshape(waves, samples, width)
    return jnp.transpose(pulled, (1, 0, 2)) + latent.astype(f32)


def solution(mesh):
    placed = (
        P(None, "wave", "event"),
        P("event", "wave"),
        P("event", None),
        P("wave", "event"),
        P("wave", "event"),
        P("wave", "event"),
        P(),
    )
    return jax.shard_map(
        functools.partial(shards, mesh.shape["event"]),
        mesh=mesh,
        in_specs=placed,
        out_specs=P(None, "wave", "event"),
        check_vma=False,
    )
```

```python
import functools
import math

import jax
import jax.numpy as jnp
from jax import lax
from jax.experimental import pallas as pl
from jax.experimental.pallas import tpu as pltpu
from jax.sharding import PartitionSpec as P

TILE = 256
LANES = 128
CHUNK = 1024
GROUP = 16
MESH = pl.DeviceIdType.MESH
NN = (((1,), (0,)), ((), ()))
NT = (((1,), (1,)), ((), ()))


def dot(a, b, dims):
    return lax.dot_general(a, b, dims, preferred_element_type=jnp.float32)


def spread_rows(dst, read, total):
    for k in range(total // LANES):
        row = read(k * LANES)
        dst[pl.ds(k * LANES, LANES), :] = jnp.broadcast_to(row, (LANES, LANES)).T


def gather_pieces(dst, src, pieces, width):
    for k in range(pieces):
        block, lane = (k * width) // TILE, (k * width) % TILE
        dst[block, :, lane : lane + width] = src(k)


def wide(column):
    return jnp.concatenate([column] * (TILE // LANES), axis=1)


def tile_pairs(blocks):
    return [(i, j) for i in range(blocks) for j in range(i, blocks)]


def add(held, term):
    return term if held is None else held + term


def multiply(sums, vec, tile, i, j):
    sums[j] = add(sums[j], dot(vec[i], tile, NN))
    if j > i:
        sums[i] = add(sums[i], dot(vec[j], tile, NT))


def scatter_pieces(dst, sums, pieces, width):
    for k in range(pieces):
        block, lane = (k * width) // TILE, (k * width) % TILE
        dst[k, 0] = sums[block][:, lane : lane + width].astype(dst.dtype)


def forward_kernel(pieces, width, coords, profile, latent, kern, amp, dist, col_l, col_g, prof, vec):
    total = pieces * width
    pairs = tile_pairs(total // TILE)
    step = 64

    @pl.when(pl.program_id(0) == 0)
    def _():
        spread_rows(col_l, lambda k: coords[0:1, k : k + LANES], total)
        spread_rows(col_g, lambda k: coords[1:2, k : k + LANES], total)

        def over_i(i, t0):
            def over_j(j, t):
                col = pl.ds(pl.multiple_of(j * TILE, TILE), TILE)
                x_c, y_c = coords[0:1, col], coords[1:2, col]
                for r in range(0, TILE, step):
                    row = pl.ds(pl.multiple_of(i * TILE + r, step), step)
                    dx = wide(col_l[row, :]) - x_c
                    dy = wide(col_g[row, :]) - y_c
                    dist[t, r : r + step, :] = (dx * dx + dy * dy) * (-math.log2(math.e))
                return t + 1

            return lax.fori_loop(i, total // TILE, over_j, t0)

        lax.fori_loop(0, total // TILE, over_i, 0)

    gather_pieces(prof, lambda k: profile[k, 0], pieces, width)
    gather_pieces(vec, lambda k: latent[k, 0], pieces, width)
    spread_rows(col_l, lambda k: prof[k // TILE, 0:1, k % TILE : k % TILE + LANES], total)
    spread_rows(col_g, lambda k: prof[k // TILE, 1:2, k % TILE : k % TILE + LANES], total)

    sums = [None] * (total // TILE)
    for t, (i, j) in enumerate(pairs):
        l_c, g_c = prof[j, 0:1, :], prof[j, 1:2, :]
        strips = []
        for r in range(0, TILE, step):
            row = pl.ds(i * TILE + r, step)
            root = lax.rsqrt(wide(col_l[row, :]) + l_c)
            power = jnp.exp2(dist[t, r : r + step, :] * (root * root))
            scale = wide(col_g[row, :]) * g_c
            strip = (scale * root * power).astype(jnp.bfloat16)
            kern[0, t, r : r + step, :] = strip
            strips.append(strip)
        multiply(sums, vec, jnp.concatenate(strips, axis=0), i, j)
    scatter_pieces(amp, sums, pieces, width)


def backward_kernel(pieces, width, kern, grad, out, vec):
    total = pieces * width
    gather_pieces(vec, lambda k: grad[k, 0], pieces, width)
    sums = [None] * (total // TILE)
    for t, (i, j) in enumerate(tile_pairs(total // TILE)):
        multiply(sums, vec, kern[0, t], i, j)
    scatter_pieces(out, sums, pieces, width)


def field_kernel(samples, inner, first, last, rows, basis, label, field):
    span = GROUP * samples
    base = pl.program_id(0) * inner

    def one(c, _):
        at = pl.ds(pl.multiple_of(c * CHUNK, CHUNK), CHUNK)
        psi = basis[at, :]
        seg = jnp.broadcast_to(label[:, at], (samples, CHUNK))

        def over_g(g, total):
            part = rows[pl.ds(pl.multiple_of(g * span, span), span), :]
            full = dot(part, psi, NT)
            own = seg - g * GROUP
            for b in range(GROUP):
                total = total + jnp.where(own == b, full[b * samples : (b + 1) * samples, :], 0.0)
            return total

        start = jnp.zeros((samples, CHUNK), jnp.float32)
        total = lax.fori_loop(first[base + c], last[base + c] + 1, over_g, start)
        field[0, :, at] = total.astype(field.dtype)
        return 0

    lax.fori_loop(0, inner, one, 0)


def sums_kernel(samples, inner, first, last, weight, basis, label, sums):
    span = GROUP * samples
    base = pl.program_id(0) * inner

    @pl.when(pl.program_id(0) == 0)
    def _():
        sums[...] = jnp.zeros_like(sums)

    def one(c, _):
        at = pl.ds(pl.multiple_of(c * CHUNK, CHUNK), CHUNK)
        psi = basis[at, :]
        seg = jnp.broadcast_to(label[:, at], (samples, CHUNK))
        value = weight[0, :, at].astype(jnp.float32)

        def over_g(g, _):
            own = seg - g * GROUP
            full = jnp.concatenate([jnp.where(own == b, value, 0.0) for b in range(GROUP)], axis=0)
            at_g = pl.ds(pl.multiple_of(g * span, span), span)
            sums[at_g, :] += dot(full.astype(jnp.bfloat16), psi, NN)
            return 0

        return lax.fori_loop(first[base + c], last[base + c] + 1, over_g, 0)

    lax.fori_loop(0, inner, one, 0)


def greet(axis, count):
    me = lax.axis_index(axis)
    peers = [lax.rem(me + d, count) for d in range(1, count)]
    barrier = pltpu.get_barrier_semaphore()
    for peer in peers:
        pl.semaphore_signal(barrier, inc=1, device_id={axis: peer}, device_id_type=MESH)
    pl.semaphore_wait(barrier, count - 1)
    return me, peers


def exchange_kernel(axis, count, arrays, *refs):
    sources, targets = refs[:arrays], refs[arrays : 2 * arrays]
    send, recv = refs[2 * arrays :]
    me, peers = greet(axis, count)
    copies = []
    for a in range(arrays):
        for d, peer in enumerate(peers):
            copy = pltpu.make_async_remote_copy(
                src_ref=sources[a].at[peer],
                dst_ref=targets[a].at[me],
                send_sem=send.at[a, d],
                recv_sem=recv.at[a, d],
                device_id={axis: peer},
                device_id_type=MESH,
            )
            copy.start()
            copies.append(copy)
    for a in range(arrays):
        targets[a][me] = sources[a][me]
    for copy in copies:
        copy.wait()


def exchange(axis, count, ident, *values):
    vmem = pl.BlockSpec(memory_space=pltpu.VMEM)
    arrays = len(values)
    return pl.pallas_call(
        functools.partial(exchange_kernel, axis, count, arrays),
        out_shape=[jax.ShapeDtypeStruct(v.shape, v.dtype) for v in values],
        in_specs=[vmem] * arrays,
        out_specs=[vmem] * arrays,
        scratch_shapes=[pltpu.SemaphoreType.DMA((arrays, count - 1))] * 2,
        compiler_params=pltpu.CompilerParams(
            collective_id=ident, has_side_effects=True, vmem_limit_bytes=8 << 20
        ),
        name=f"exchange_{ident}",
    )(*values)


def weight_kernel(axis, count, samples, partial, weight, landed, made, send, recv, local):
    me, peers = greet(axis, count)
    copies = []
    for d, peer in enumerate(peers):
        copy = pltpu.make_async_remote_copy(
            src_ref=partial.at[peer],
            dst_ref=landed.at[d],
            send_sem=send.at[0, d],
            recv_sem=recv.at[0, d],
            device_id={axis: peer},
            device_id_type=MESH,
        )
        copy.start()
        copies.append(copy)
    for copy in copies:
        copy.wait()
    total = partial[me].astype(jnp.float32)
    for d in range(count - 1):
        total = total + landed[d].astype(jnp.float32)
    made[...] = (-2.0 * total / (1.0 + total * total) / samples).astype(made.dtype)
    keep = pltpu.make_async_copy(made, weight.at[me], local)
    keep.start()
    keep.wait()
    copies = []
    for d, peer in enumerate(peers):
        copy = pltpu.make_async_remote_copy(
            src_ref=weight.at[me],
            dst_ref=weight.at[me],
            send_sem=send.at[1, d],
            recv_sem=recv.at[1, d],
            device_id={axis: peer},
            device_id_type=MESH,
        )
        copy.start()
        copies.append(copy)
    for copy in copies:
        copy.wait()


def share_weight(axis, count, ident, samples, partial):
    vmem = pl.BlockSpec(memory_space=pltpu.VMEM)
    shape, dtype = partial.shape, partial.dtype
    return pl.pallas_call(
        functools.partial(weight_kernel, axis, count, samples),
        out_shape=jax.ShapeDtypeStruct(shape, dtype),
        in_specs=[vmem],
        out_specs=vmem,
        scratch_shapes=[
            pltpu.VMEM((count - 1,) + shape[1:], dtype),
            pltpu.VMEM(shape[1:], dtype),
            pltpu.SemaphoreType.DMA((2, count - 1)),
            pltpu.SemaphoreType.DMA((2, count - 1)),
            pltpu.SemaphoreType.DMA,
        ],
        compiler_params=pltpu.CompilerParams(
            collective_id=ident, has_side_effects=True, vmem_limit_bytes=12 << 20
        ),
        name="share_weight",
    )(partial)


def params(limit=60 << 20):
    return pltpu.CompilerParams(dimension_semantics=("arbitrary",), vmem_limit_bytes=limit)


def shards(count, splits, latent, basis, event_bin, length, amplitude_scale, yield_norm, bin_coords):
    samples, waves, width = latent.shape
    total = bin_coords.shape[1]
    own = waves // count
    blocks = total // TILE
    tiles = blocks * (blocks + 1) // 2
    f32, bf16 = jnp.float32, jnp.bfloat16

    profile = jnp.stack(
        [length * length, amplitude_scale * jnp.sqrt(math.sqrt(2.0) * length)], axis=1
    ).reshape(count, own, 2, width)
    draws = jnp.transpose(latent, (1, 0, 2)).reshape(count, own, samples, width)
    profile, draws = exchange("event", count, 0, profile, draws)

    piece = pl.BlockSpec((count, 1, samples, width), lambda w: (0, w, 0, 0))
    kern_spec = pl.BlockSpec((1, tiles, TILE, TILE), lambda w: (w, 0, 0, 0))
    kern, amp = pl.pallas_call(
        functools.partial(forward_kernel, count, width),
        out_shape=(
            jax.ShapeDtypeStruct((own, tiles, TILE, TILE), bf16),
            jax.ShapeDtypeStruct((count, own, samples, width), bf16),
        ),
        grid=(own,),
        in_specs=[
            pl.BlockSpec((2, total), lambda w: (0, 0)),
            pl.BlockSpec((count, 1, 2, width), lambda w: (0, w, 0, 0)),
            piece,
        ],
        out_specs=(kern_spec, piece),
        scratch_shapes=[
            pltpu.VMEM((tiles, TILE, TILE), f32),
            pltpu.VMEM((total, LANES), f32),
            pltpu.VMEM((total, LANES), f32),
            pltpu.VMEM((blocks, 2, TILE), f32),
            pltpu.VMEM((blocks, samples, TILE), bf16),
        ],
        compiler_params=params(),
        name="kern_forward",
    )(bin_coords, profile, draws)

    (amp,) = exchange("event", count, 1, amp)
    amp = amp.reshape(waves, samples, width)
    amp_rows = jnp.transpose(amp, (2, 1, 0)).reshape(width * samples, waves)

    events = basis.shape[0]
    block = min(events // splits, 4096)
    per = events // splits // block
    inner = block // CHUNK
    grouped = event_bin.reshape(events // CHUNK, CHUNK) // GROUP
    first, last = grouped[:, 0], grouped[:, -1]
    basis_spec = pl.BlockSpec((block, waves), lambda e, *_: (e, 0))
    label_spec = pl.BlockSpec((1, block), lambda e, *_: (0, e))
    field_spec = pl.BlockSpec((1, samples, block), lambda e, *_: (e // per, 0, e % per))
    rows_spec = pl.BlockSpec((width * samples, waves), lambda e, *_: (0, 0))
    field = pl.pallas_call(
        functools.partial(field_kernel, samples, inner),
        out_shape=jax.ShapeDtypeStruct((splits, samples, events // splits), bf16),
        grid_spec=pltpu.PrefetchScalarGridSpec(
            num_scalar_prefetch=2,
            grid=(events // block,),
            in_specs=[rows_spec, basis_spec, label_spec],
            out_specs=field_spec,
        ),
        compiler_params=params(),
        name="event_field",
    )(first, last, amp_rows, basis, event_bin)
    weight = share_weight("wave", splits, 2, samples, field)
    sums = pl.pallas_call(
        functools.partial(sums_kernel, samples, inner),
        out_shape=jax.ShapeDtypeStruct((width * samples, waves), f32),
        grid_spec=pltpu.PrefetchScalarGridSpec(
            num_scalar_prefetch=2,
            grid=(events // block,),
            in_specs=[field_spec, basis_spec, label_spec],
            out_specs=rows_spec,
        ),
        compiler_params=params(),
        name="event_sums",
    )(first, last, weight, basis, event_bin)

    sums = jnp.transpose(sums.reshape(width, samples, waves), (2, 1, 0))
    grad = (sums + 2.0 / samples * amp.astype(f32) * yield_norm[:, None, :]).astype(bf16)
    (grad,) = exchange("event", count, 3, grad.reshape(count, own, samples, width))
    pulled = pl.pallas_call(
        functools.partial(backward_kernel, count, width),
        out_shape=jax.ShapeDtypeStruct((count, own, samples, width), bf16),
        grid=(own,),
        in_specs=[kern_spec, piece],
        out_specs=piece,
        scratch_shapes=[
            pltpu.VMEM((blocks, samples, TILE), bf16),
        ],
        compiler_params=params(),
        name="kern_backward",
    )(kern, grad)
    (pulled,) = exchange("event", count, 4, pulled)
    pulled = pulled.reshape(waves, samples, width).astype(f32)
    return jnp.transpose(pulled, (1, 0, 2)) + latent.astype(f32)


def solution(mesh):
    placed = (
        P(None, "wave", "event"),
        P("event", "wave"),
        P("event", None),
        P("wave", "event"),
        P("wave", "event"),
        P("wave", "event"),
        P(),
    )
    return jax.shard_map(
        functools.partial(shards, mesh.shape["event"], mesh.shape["wave"]),
        mesh=mesh,
        in_specs=placed,
        out_specs=P(None, "wave", "event"),
        check_vma=False,
    )
```

```python
import functools
import math

import jax
import jax.numpy as jnp
from jax import lax
from jax.experimental import pallas as pl
from jax.experimental.pallas import tpu as pltpu
from jax.sharding import PartitionSpec as P

TILE = 256
LANES = 128
CHUNK = 1024
GROUP = 16
BATCHES = 4
MESH = pl.DeviceIdType.MESH
NN = (((1,), (0,)), ((), ()))
NT = (((1,), (1,)), ((), ()))


def dot(a, b, dims):
    return lax.dot_general(a, b, dims, preferred_element_type=jnp.float32)


def spread_rows(dst, read, total):
    for k in range(total // LANES):
        row = read(k * LANES)
        dst[pl.ds(k * LANES, LANES), :] = jnp.broadcast_to(row, (LANES, LANES)).T


def gather_pieces(dst, src, pieces, width):
    for k in range(pieces):
        block, lane = (k * width) // TILE, (k * width) % TILE
        dst[block, :, lane : lane + width] = src(k)


def wide(column):
    return jnp.concatenate([column] * (TILE // LANES), axis=1)


def tile_pairs(blocks):
    return [(i, j) for i in range(blocks) for j in range(i, blocks)]


def add(held, term):
    return term if held is None else held + term


def multiply(sums, vec, tile, i, j):
    sums[j] = add(sums[j], dot(vec[i], tile, NN))
    if j > i:
        sums[i] = add(sums[i], dot(vec[j], tile, NT))


def keep_pieces(dst, slot, sums, pieces, width):
    for k in range(pieces):
        block, lane = (k * width) // TILE, (k * width) % TILE
        dst[slot, k] = sums[block][:, lane : lane + width].astype(dst.dtype)


def around(axis, count):
    me = lax.axis_index(axis)
    return me, [lax.rem(me + d, count) for d in range(1, count)]


def remote(axis, peer, src, dst, send, recv):
    return pltpu.make_async_remote_copy(
        src_ref=src,
        dst_ref=dst,
        send_sem=send,
        recv_sem=recv,
        device_id={axis: peer},
        device_id_type=MESH,
    )


def inward(axis, count, batch, sources, targets, send, recv):
    me, peers = around(axis, count)

    def copies(q):
        size = sources[0].shape[1] // batch
        at = pl.ds(q * size, size)
        return [
            remote(axis, peer, src.at[peer, at], dst.at[me, at], send.at[a, q, d], recv.at[a, q, d])
            for a, (src, dst) in enumerate(zip(sources, targets))
            for d, peer in enumerate(peers)
        ]

    return copies


def outward(axis, count, stage, landed, send, recv):
    me, peers = around(axis, count)

    def copies(w):
        return [
            remote(axis, peer, stage.at[w, peer], landed.at[me, w], send.at[w, d], recv.at[w, d])
            for d, peer in enumerate(peers)
        ]

    return copies


def open_batches(axis, count, batch, sources, targets, copies):
    me, _ = greet(axis, count)
    for q in range(batch):
        for copy in copies(q):
            copy.start()
    for src, dst in zip(sources, targets):
        dst[me] = src[me]


def close_all(own, batch, copies_in, copies_out):
    def sent(q, _):
        for copy in copies_in(q):
            copy.wait_send()
        return 0

    def done(w, _):
        for copy in copies_out(w):
            copy.wait()
        return 0

    lax.fori_loop(0, batch, sent, 0)
    lax.fori_loop(0, own, done, 0)


def forward_kernel(
    axis, pieces, width, own, batch,
    coords, profile, latent, kern, amp,
    dist, col_l, col_g, prof, vec, prof_all, draws_all, stage, landed,
    in_send, in_recv, out_send, out_recv,
):
    total = pieces * width
    pairs = tile_pairs(total // TILE)
    step = 64
    w = pl.program_id(0)
    sources, targets = (profile, latent), (prof_all, draws_all)
    copies_in = inward(axis, pieces, batch, sources, targets, in_send, in_recv)
    copies_out = outward(axis, pieces, stage, landed, out_send, out_recv)
    me = lax.axis_index(axis)

    @pl.when(w == 0)
    def _():
        open_batches(axis, pieces, batch, sources, targets, copies_in)
        spread_rows(col_l, lambda k: coords[0:1, k : k + LANES], total)
        spread_rows(col_g, lambda k: coords[1:2, k : k + LANES], total)

        def over_i(i, t0):
            def over_j(j, t):
                col = pl.ds(pl.multiple_of(j * TILE, TILE), TILE)
                x_c, y_c = coords[0:1, col], coords[1:2, col]
                for r in range(0, TILE, step):
                    row = pl.ds(pl.multiple_of(i * TILE + r, step), step)
                    dx = wide(col_l[row, :]) - x_c
                    dy = wide(col_g[row, :]) - y_c
                    dist[t, r : r + step, :] = (dx * dx + dy * dy) * (-math.log2(math.e))
                return t + 1

            return lax.fori_loop(i, total // TILE, over_j, t0)

        lax.fori_loop(0, total // TILE, over_i, 0)

    @pl.when(w > 0)
    def _():
        for copy in copies_out(w - 1):
            copy.start()
        landed[me, w - 1] = stage[w - 1, me]

    @pl.when(jnp.logical_and(w < own, lax.rem(w, own // batch) == 0))
    def _():
        for copy in copies_in(w // (own // batch)):
            copy.wait_recv()

    @pl.when(w < own)
    def _():
        gather_pieces(prof, lambda k: prof_all[k, w], pieces, width)
        gather_pieces(vec, lambda k: draws_all[k, w], pieces, width)
        spread_rows(col_l, lambda k: prof[k // TILE, 0:1, k % TILE : k % TILE + LANES], total)
        spread_rows(col_g, lambda k: prof[k // TILE, 1:2, k % TILE : k % TILE + LANES], total)
        sums = [None] * (total // TILE)
        for t, (i, j) in enumerate(pairs):
            l_c, g_c = prof[j, 0:1, :], prof[j, 1:2, :]
            strips = []
            for r in range(0, TILE, step):
                row = pl.ds(i * TILE + r, step)
                root = lax.rsqrt(wide(col_l[row, :]) + l_c)
                power = jnp.exp2(dist[t, r : r + step, :] * (root * root))
                scale = wide(col_g[row, :]) * g_c
                strip = (scale * root * power).astype(jnp.bfloat16)
                kern[0, t, r : r + step, :] = strip
                strips.append(strip)
            multiply(sums, vec, jnp.concatenate(strips, axis=0), i, j)
        keep_pieces(stage, w, sums, pieces, width)

    @pl.when(w == own)
    def _():
        close_all(own, batch, copies_in, copies_out)
        amp[...] = landed[...]


def backward_kernel(
    axis, pieces, width, own, batch,
    kern, grad, out,
    vec, grad_all, stage, landed, in_send, in_recv, out_send, out_recv,
):
    total = pieces * width
    w = pl.program_id(0)
    copies_in = inward(axis, pieces, batch, (grad,), (grad_all,), in_send, in_recv)
    copies_out = outward(axis, pieces, stage, landed, out_send, out_recv)
    me = lax.axis_index(axis)

    @pl.when(w == 0)
    def _():
        open_batches(axis, pieces, batch, (grad,), (grad_all,), copies_in)

    @pl.when(w > 0)
    def _():
        for copy in copies_out(w - 1):
            copy.start()
        landed[me, w - 1] = stage[w - 1, me]

    @pl.when(jnp.logical_and(w < own, lax.rem(w, own // batch) == 0))
    def _():
        for copy in copies_in(w // (own // batch)):
            copy.wait_recv()

    @pl.when(w < own)
    def _():
        gather_pieces(vec, lambda k: grad_all[k, w], pieces, width)
        sums = [None] * (total // TILE)
        for t, (i, j) in enumerate(tile_pairs(total // TILE)):
            multiply(sums, vec, kern[0, t], i, j)
        keep_pieces(stage, w, sums, pieces, width)

    @pl.when(w == own)
    def _():
        close_all(own, batch, copies_in, copies_out)
        out[...] = landed[...]


def field_kernel(samples, inner, first, last, rows, basis, label, field):
    base = pl.program_id(0) * inner

    def group(c, start):
        at = pl.ds(c * CHUNK, CHUNK)
        part = rows[pl.ds(pl.multiple_of(start * samples, 2 * samples), GROUP * samples), :]
        full = dot(part, basis[at, :], NT)
        own = jnp.broadcast_to(label[:, at], (samples, CHUNK)) - start
        total = jnp.zeros((samples, CHUNK), jnp.float32)
        for b in range(GROUP):
            total = total + jnp.where(own == b, full[b * samples : (b + 1) * samples, :], 0.0)
        return total

    starts = [first[base + c] // 2 * 2 for c in range(inner)]
    totals = [group(c, starts[c]) for c in range(inner)]
    for c in range(inner):
        trips = (last[base + c] - starts[c]) // GROUP + 1

        def over(k, total, c=c):
            return total + group(c, starts[c] + k * GROUP)

        total = lax.fori_loop(1, trips, over, totals[c])
        field[0, :, c * CHUNK : (c + 1) * CHUNK] = total.astype(field.dtype)


def sums_kernel(samples, inner, first, last, weight, basis, label, sums):
    base = pl.program_id(0) * inner

    @pl.when(pl.program_id(0) == 0)
    def _():
        sums[...] = jnp.zeros_like(sums)

    def group(c, start):
        at = pl.ds(c * CHUNK, CHUNK)
        own = jnp.broadcast_to(label[:, at], (samples, CHUNK)) - start
        value = weight[0, :, at].astype(jnp.float32)
        full = jnp.concatenate([jnp.where(own == b, value, 0.0) for b in range(GROUP)], axis=0)
        return dot(full.astype(jnp.bfloat16), basis[at, :], NN)

    def put(start, term):
        sums[pl.ds(pl.multiple_of(start * samples, 2 * samples), GROUP * samples), :] += term

    starts = [first[base + c] // 2 * 2 for c in range(inner)]
    terms = [group(c, starts[c]) for c in range(inner)]
    for c in range(inner):
        put(starts[c], terms[c])
    for c in range(inner):
        trips = (last[base + c] - starts[c]) // GROUP + 1

        def over(k, _, c=c):
            put(starts[c] + k * GROUP, group(c, starts[c] + k * GROUP))
            return 0

        lax.fori_loop(1, trips, over, 0)


def greet(axis, count):
    me = lax.axis_index(axis)
    peers = [lax.rem(me + d, count) for d in range(1, count)]
    barrier = pltpu.get_barrier_semaphore()
    for peer in peers:
        pl.semaphore_signal(barrier, inc=1, device_id={axis: peer}, device_id_type=MESH)
    pl.semaphore_wait(barrier, count - 1)
    return me, peers


def weight_kernel(axis, count, samples, partial, weight, landed, made, send, recv, local):
    me, peers = greet(axis, count)
    copies = []
    for d, peer in enumerate(peers):
        copy = pltpu.make_async_remote_copy(
            src_ref=partial.at[peer],
            dst_ref=landed.at[d],
            send_sem=send.at[0, d],
            recv_sem=recv.at[0, d],
            device_id={axis: peer},
            device_id_type=MESH,
        )
        copy.start()
        copies.append(copy)
    for copy in copies:
        copy.wait()
    total = partial[me].astype(jnp.float32)
    for d in range(count - 1):
        total = total + landed[d].astype(jnp.float32)
    made[...] = (-2.0 * total / (1.0 + total * total) / samples).astype(made.dtype)
    keep = pltpu.make_async_copy(made, weight.at[me], local)
    keep.start()
    keep.wait()
    copies = []
    for d, peer in enumerate(peers):
        copy = pltpu.make_async_remote_copy(
            src_ref=weight.at[me],
            dst_ref=weight.at[me],
            send_sem=send.at[1, d],
            recv_sem=recv.at[1, d],
            device_id={axis: peer},
            device_id_type=MESH,
        )
        copy.start()
        copies.append(copy)
    for copy in copies:
        copy.wait()


def share_weight(axis, count, ident, samples, partial):
    vmem = pl.BlockSpec(memory_space=pltpu.VMEM)
    shape, dtype = partial.shape, partial.dtype
    return pl.pallas_call(
        functools.partial(weight_kernel, axis, count, samples),
        out_shape=jax.ShapeDtypeStruct(shape, dtype),
        in_specs=[vmem],
        out_specs=vmem,
        scratch_shapes=[
            pltpu.VMEM((count - 1,) + shape[1:], dtype),
            pltpu.VMEM(shape[1:], dtype),
            pltpu.SemaphoreType.DMA((2, count - 1)),
            pltpu.SemaphoreType.DMA((2, count - 1)),
            pltpu.SemaphoreType.DMA,
        ],
        compiler_params=pltpu.CompilerParams(
            collective_id=ident, has_side_effects=True, vmem_limit_bytes=12 << 20
        ),
        name="share_weight",
    )(partial)


def params(**more):
    return pltpu.CompilerParams(
        dimension_semantics=("arbitrary",), vmem_limit_bytes=60 << 20, **more
    )


def shards(count, splits, latent, basis, event_bin, length, amplitude_scale, yield_norm, bin_coords):
    samples, waves, width = latent.shape
    total = bin_coords.shape[1]
    own = waves // count
    blocks = total // TILE
    tiles = blocks * (blocks + 1) // 2
    f32, bf16 = jnp.float32, jnp.bfloat16

    profile = jnp.stack(
        [length * length, amplitude_scale * jnp.sqrt(math.sqrt(2.0) * length)], axis=1
    ).reshape(count, own, 2, width)
    draws = jnp.transpose(latent, (1, 0, 2)).reshape(count, own, samples, width)

    batch = math.gcd(own, BATCHES)
    vmem = pl.BlockSpec(memory_space=pltpu.VMEM)
    piece = jax.ShapeDtypeStruct((count, own, samples, width), bf16)
    kern_spec = pl.BlockSpec((1, tiles, TILE, TILE), lambda w: (jnp.minimum(w, own - 1), 0, 0, 0))
    stages = [
        pltpu.VMEM((own, count, samples, width), bf16),
        pltpu.VMEM((count, own, samples, width), bf16),
    ]

    def semaphores(arrays):
        return [pltpu.SemaphoreType.DMA((arrays, batch, count - 1))] * 2 + [
            pltpu.SemaphoreType.DMA((own, count - 1))
        ] * 2

    kern, amp = pl.pallas_call(
        functools.partial(forward_kernel, "event", count, width, own, batch),
        out_shape=(jax.ShapeDtypeStruct((own, tiles, TILE, TILE), bf16), piece),
        grid=(own + 1,),
        in_specs=[vmem, vmem, vmem],
        out_specs=(kern_spec, vmem),
        scratch_shapes=[
            pltpu.VMEM((tiles, TILE, TILE), f32),
            pltpu.VMEM((total, LANES), f32),
            pltpu.VMEM((total, LANES), f32),
            pltpu.VMEM((blocks, 2, TILE), f32),
            pltpu.VMEM((blocks, samples, TILE), bf16),
            pltpu.VMEM((count, own, 2, width), f32),
            pltpu.VMEM((count, own, samples, width), bf16),
        ]
        + stages
        + semaphores(2),
        compiler_params=params(collective_id=0, has_side_effects=True),
        name="kern_forward",
    )(bin_coords, profile, draws)

    amp = amp.reshape(waves, samples, width)
    amp_rows = jnp.transpose(amp, (2, 1, 0)).reshape(width * samples, waves)
    amp_rows = jnp.pad(amp_rows, ((0, GROUP * samples), (0, 0)))

    events = basis.shape[0]
    block = min(events // splits, 4096)
    per = events // splits // block
    inner = block // CHUNK
    grouped = event_bin.reshape(events // CHUNK, CHUNK)
    first, last = grouped[:, 0], grouped[:, -1]
    basis_spec = pl.BlockSpec((block, waves), lambda e, *_: (e, 0))
    label_spec = pl.BlockSpec((1, block), lambda e, *_: (0, e))
    field_spec = pl.BlockSpec((1, samples, block), lambda e, *_: (e // per, 0, e % per))
    rows_spec = pl.BlockSpec(((width + GROUP) * samples, waves), lambda e, *_: (0, 0))
    field = pl.pallas_call(
        functools.partial(field_kernel, samples, inner),
        out_shape=jax.ShapeDtypeStruct((splits, samples, events // splits), bf16),
        grid_spec=pltpu.PrefetchScalarGridSpec(
            num_scalar_prefetch=2,
            grid=(events // block,),
            in_specs=[rows_spec, basis_spec, label_spec],
            out_specs=field_spec,
        ),
        compiler_params=params(),
        name="event_field",
    )(first, last, amp_rows, basis, event_bin)
    weight = share_weight("wave", splits, 2, samples, field)
    sums = pl.pallas_call(
        functools.partial(sums_kernel, samples, inner),
        out_shape=jax.ShapeDtypeStruct(((width + GROUP) * samples, waves), f32),
        grid_spec=pltpu.PrefetchScalarGridSpec(
            num_scalar_prefetch=2,
            grid=(events // block,),
            in_specs=[field_spec, basis_spec, label_spec],
            out_specs=rows_spec,
        ),
        compiler_params=params(),
        name="event_sums",
    )(first, last, weight, basis, event_bin)

    sums = jnp.transpose(sums[: width * samples].reshape(width, samples, waves), (2, 1, 0))
    grad = (sums + 2.0 / samples * amp.astype(f32) * yield_norm[:, None, :]).astype(bf16)
    pulled = pl.pallas_call(
        functools.partial(backward_kernel, "event", count, width, own, batch),
        out_shape=piece,
        grid=(own + 1,),
        in_specs=[kern_spec, vmem],
        out_specs=vmem,
        scratch_shapes=[
            pltpu.VMEM((blocks, samples, TILE), bf16),
            pltpu.VMEM((count, own, samples, width), bf16),
        ]
        + stages
        + semaphores(1),
        compiler_params=params(collective_id=1, has_side_effects=True),
        name="kern_backward",
    )(kern, grad.reshape(count, own, samples, width))
    pulled = pulled.reshape(waves, samples, width).astype(f32)
    return jnp.transpose(pulled, (1, 0, 2)) + latent.astype(f32)


def solution(mesh):
    placed = (
        P(None, "wave", "event"),
        P("event", "wave"),
        P("event", None),
        P("wave", "event"),
        P("wave", "event"),
        P("wave", "event"),
        P(),
    )
    return jax.shard_map(
        functools.partial(shards, mesh.shape["event"], mesh.shape["wave"]),
        mesh=mesh,
        in_specs=placed,
        out_specs=P(None, "wave", "event"),
        check_vma=False,
    )
```

```python
import functools
import math

import jax
import jax.numpy as jnp
from jax import lax
from jax.experimental import pallas as pl
from jax.experimental.pallas import tpu as pltpu
from jax.sharding import PartitionSpec as P

TILE = 256
LANES = 128
CHUNK = 1024
GROUP = 16
BATCHES = 8
MESH = pl.DeviceIdType.MESH
NN = (((1,), (0,)), ((), ()))
NT = (((1,), (1,)), ((), ()))


def dot(a, b, dims):
    return lax.dot_general(a, b, dims, preferred_element_type=jnp.float32)


def spread_rows(dst, read, total):
    for k in range(total // LANES):
        row = read(k * LANES)
        dst[pl.ds(k * LANES, LANES), :] = jnp.broadcast_to(row, (LANES, LANES)).T


def gather_pieces(dst, src, pieces, width):
    for k in range(pieces):
        block, lane = (k * width) // TILE, (k * width) % TILE
        dst[block, :, lane : lane + width] = src(k)


def wide(column):
    return jnp.concatenate([column] * (TILE // LANES), axis=1)


def tile_pairs(blocks):
    return [(i, j) for i in range(blocks) for j in range(i, blocks)]


def add(held, term):
    return term if held is None else held + term


def multiply(sums, vec, tile, i, j):
    sums[j] = add(sums[j], dot(vec[i], tile, NN))
    if j > i:
        sums[i] = add(sums[i], dot(vec[j], tile, NT))


def keep_pieces(dst, slot, sums, pieces, width):
    for k in range(pieces):
        block, lane = (k * width) // TILE, (k * width) % TILE
        dst[slot, k] = sums[block][:, lane : lane + width].astype(dst.dtype)


def around(axis, count):
    me = lax.axis_index(axis)
    return me, [lax.rem(me + d, count) for d in range(1, count)]


def remote(axis, peer, src, dst, send, recv):
    return pltpu.make_async_remote_copy(
        src_ref=src,
        dst_ref=dst,
        send_sem=send,
        recv_sem=recv,
        device_id={axis: peer},
        device_id_type=MESH,
    )


def inward(axis, count, batch, sources, targets, send, recv):
    me, peers = around(axis, count)

    def copies(q):
        size = sources[0].shape[1] // batch
        at = pl.ds(q * size, size)
        return [
            remote(axis, peer, src.at[peer, at], dst.at[me, at], send.at[a, q, d], recv.at[a, q, d])
            for a, (src, dst) in enumerate(zip(sources, targets))
            for d, peer in enumerate(peers)
        ]

    return copies


def outward(axis, count, stage, landed, send, recv):
    me, peers = around(axis, count)

    def copies(w):
        return [
            remote(axis, peer, stage.at[w, peer], landed.at[me, w], send.at[w, d], recv.at[w, d])
            for d, peer in enumerate(peers)
        ]

    return copies


def open_batches(axis, count, batch, sources, targets, copies):
    me, _ = greet(axis, count)
    for q in range(batch):
        for copy in copies(q):
            copy.start()
    for src, dst in zip(sources, targets):
        dst[me] = src[me]


def close_all(own, batch, copies_in, copies_out):
    def sent(q, _):
        for copy in copies_in(q):
            copy.wait_send()
        return 0

    def done(w, _):
        for copy in copies_out(w):
            copy.wait()
        return 0

    lax.fori_loop(0, batch, sent, 0)
    lax.fori_loop(0, own, done, 0)


def forward_kernel(
    axis, pieces, width, own, batch,
    coords, profile, latent, kern, amp,
    dist, col_l, col_g, prof, vec, prof_all, draws_all, stage, landed,
    in_send, in_recv, out_send, out_recv,
):
    total = pieces * width
    pairs = tile_pairs(total // TILE)
    step = 64
    w = pl.program_id(0)
    sources, targets = (profile, latent), (prof_all, draws_all)
    copies_in = inward(axis, pieces, batch, sources, targets, in_send, in_recv)
    copies_out = outward(axis, pieces, stage, landed, out_send, out_recv)
    me = lax.axis_index(axis)

    @pl.when(w == 0)
    def _():
        open_batches(axis, pieces, batch, sources, targets, copies_in)
        spread_rows(col_l, lambda k: coords[0:1, k : k + LANES], total)
        spread_rows(col_g, lambda k: coords[1:2, k : k + LANES], total)

        def over_i(i, t0):
            def over_j(j, t):
                col = pl.ds(pl.multiple_of(j * TILE, TILE), TILE)
                x_c, y_c = coords[0:1, col], coords[1:2, col]
                for r in range(0, TILE, step):
                    row = pl.ds(pl.multiple_of(i * TILE + r, step), step)
                    dx = wide(col_l[row, :]) - x_c
                    dy = wide(col_g[row, :]) - y_c
                    dist[t, r : r + step, :] = (dx * dx + dy * dy) * (-math.log2(math.e))
                return t + 1

            return lax.fori_loop(i, total // TILE, over_j, t0)

        lax.fori_loop(0, total // TILE, over_i, 0)

    @pl.when(w > 0)
    def _():
        for copy in copies_out(w - 1):
            copy.start()
        landed[me, w - 1] = stage[w - 1, me]

    @pl.when(jnp.logical_and(w < own, lax.rem(w, own // batch) == 0))
    def _():
        for copy in copies_in(w // (own // batch)):
            copy.wait_recv()

    @pl.when(w < own)
    def _():
        gather_pieces(prof, lambda k: prof_all[k, w], pieces, width)
        gather_pieces(vec, lambda k: draws_all[k, w], pieces, width)
        spread_rows(col_l, lambda k: prof[k // TILE, 0:1, k % TILE : k % TILE + LANES], total)
        spread_rows(col_g, lambda k: prof[k // TILE, 1:2, k % TILE : k % TILE + LANES], total)
        sums = [None] * (total // TILE)
        for t, (i, j) in enumerate(pairs):
            l_c, g_c = prof[j, 0:1, :], prof[j, 1:2, :]
            strips = []
            for r in range(0, TILE, step):
                row = pl.ds(i * TILE + r, step)
                root = lax.rsqrt(wide(col_l[row, :]) + l_c)
                power = jnp.exp2(dist[t, r : r + step, :] * (root * root))
                scale = wide(col_g[row, :]) * g_c
                strip = (scale * root * power).astype(jnp.bfloat16)
                kern[0, t, r : r + step, :] = strip
                strips.append(strip)
            multiply(sums, vec, jnp.concatenate(strips, axis=0), i, j)
        keep_pieces(stage, w, sums, pieces, width)

    @pl.when(w == own)
    def _():
        close_all(own, batch, copies_in, copies_out)
        amp[...] = landed[...]


def backward_kernel(
    axis, pieces, width, own, batch,
    kern, grad, out,
    vec, grad_all, stage, landed, in_send, in_recv, out_send, out_recv,
):
    total = pieces * width
    w = pl.program_id(0)
    copies_in = inward(axis, pieces, batch, (grad,), (grad_all,), in_send, in_recv)
    copies_out = outward(axis, pieces, stage, landed, out_send, out_recv)
    me = lax.axis_index(axis)

    @pl.when(w == 0)
    def _():
        open_batches(axis, pieces, batch, (grad,), (grad_all,), copies_in)

    @pl.when(w > 0)
    def _():
        for copy in copies_out(w - 1):
            copy.start()
        landed[me, w - 1] = stage[w - 1, me]

    @pl.when(jnp.logical_and(w < own, lax.rem(w, own // batch) == 0))
    def _():
        for copy in copies_in(w // (own // batch)):
            copy.wait_recv()

    @pl.when(w < own)
    def _():
        gather_pieces(vec, lambda k: grad_all[k, w], pieces, width)
        sums = [None] * (total // TILE)
        for t, (i, j) in enumerate(tile_pairs(total // TILE)):
            multiply(sums, vec, kern[0, t], i, j)
        keep_pieces(stage, w, sums, pieces, width)

    @pl.when(w == own)
    def _():
        close_all(own, batch, copies_in, copies_out)
        out[...] = landed[...]


def field_kernel(samples, inner, first, last, rows, basis, label, field):
    base = pl.program_id(0) * inner

    def group(c, start):
        at = pl.ds(c * CHUNK, CHUNK)
        part = rows[pl.ds(pl.multiple_of(start * samples, 2 * samples), GROUP * samples), :]
        full = dot(part, basis[at, :], NT)
        own = jnp.broadcast_to(label[:, at], (samples, CHUNK)) - start
        total = jnp.zeros((samples, CHUNK), jnp.float32)
        for b in range(GROUP):
            total = total + jnp.where(own == b, full[b * samples : (b + 1) * samples, :], 0.0)
        return total

    starts = [first[base + c] // 2 * 2 for c in range(inner)]
    totals = [group(c, starts[c]) for c in range(inner)]
    for c in range(inner):
        trips = (last[base + c] - starts[c]) // GROUP + 1

        def over(k, total, c=c):
            return total + group(c, starts[c] + k * GROUP)

        total = lax.fori_loop(1, trips, over, totals[c])
        field[0, :, c * CHUNK : (c + 1) * CHUNK] = total.astype(field.dtype)


def sums_kernel(samples, inner, first, last, weight, basis, label, sums):
    base = pl.program_id(0) * inner

    @pl.when(pl.program_id(0) == 0)
    def _():
        sums[...] = jnp.zeros_like(sums)

    def group(c, start):
        at = pl.ds(c * CHUNK, CHUNK)
        own = jnp.broadcast_to(label[:, at], (samples, CHUNK)) - start
        value = weight[0, :, at].astype(jnp.float32)
        full = jnp.concatenate([jnp.where(own == b, value, 0.0) for b in range(GROUP)], axis=0)
        return dot(full.astype(jnp.bfloat16), basis[at, :], NN)

    def put(start, term):
        sums[pl.ds(pl.multiple_of(start * samples, 2 * samples), GROUP * samples), :] += term

    starts = [first[base + c] // 2 * 2 for c in range(inner)]
    terms = [group(c, starts[c]) for c in range(inner)]
    for c in range(inner):
        put(starts[c], terms[c])
    for c in range(inner):
        trips = (last[base + c] - starts[c]) // GROUP + 1

        def over(k, _, c=c):
            put(starts[c] + k * GROUP, group(c, starts[c] + k * GROUP))
            return 0

        lax.fori_loop(1, trips, over, 0)


def greet(axis, count):
    me = lax.axis_index(axis)
    peers = [lax.rem(me + d, count) for d in range(1, count)]
    barrier = pltpu.get_barrier_semaphore()
    for peer in peers:
        pl.semaphore_signal(barrier, inc=1, device_id={axis: peer}, device_id_type=MESH)
    pl.semaphore_wait(barrier, count - 1)
    return me, peers


def weight_kernel(axis, count, samples, partial, weight, landed, made, send, recv, local):
    me, peers = greet(axis, count)
    copies = []
    for d, peer in enumerate(peers):
        copy = pltpu.make_async_remote_copy(
            src_ref=partial.at[peer],
            dst_ref=landed.at[d],
            send_sem=send.at[0, d],
            recv_sem=recv.at[0, d],
            device_id={axis: peer},
            device_id_type=MESH,
        )
        copy.start()
        copies.append(copy)
    for copy in copies:
        copy.wait()
    total = partial[me].astype(jnp.float32)
    for d in range(count - 1):
        total = total + landed[d].astype(jnp.float32)
    made[...] = (-2.0 * total / (1.0 + total * total) / samples).astype(made.dtype)
    keep = pltpu.make_async_copy(made, weight.at[me], local)
    keep.start()
    keep.wait()
    copies = []
    for d, peer in enumerate(peers):
        copy = pltpu.make_async_remote_copy(
            src_ref=weight.at[me],
            dst_ref=weight.at[me],
            send_sem=send.at[1, d],
            recv_sem=recv.at[1, d],
            device_id={axis: peer},
            device_id_type=MESH,
        )
        copy.start()
        copies.append(copy)
    for copy in copies:
        copy.wait()


def share_weight(axis, count, ident, samples, partial):
    vmem = pl.BlockSpec(memory_space=pltpu.VMEM)
    shape, dtype = partial.shape, partial.dtype
    return pl.pallas_call(
        functools.partial(weight_kernel, axis, count, samples),
        out_shape=jax.ShapeDtypeStruct(shape, dtype),
        in_specs=[vmem],
        out_specs=vmem,
        scratch_shapes=[
            pltpu.VMEM((count - 1,) + shape[1:], dtype),
            pltpu.VMEM(shape[1:], dtype),
            pltpu.SemaphoreType.DMA((2, count - 1)),
            pltpu.SemaphoreType.DMA((2, count - 1)),
            pltpu.SemaphoreType.DMA,
        ],
        compiler_params=pltpu.CompilerParams(
            collective_id=ident, has_side_effects=True, vmem_limit_bytes=12 << 20
        ),
        name="share_weight",
    )(partial)


def params(**more):
    return pltpu.CompilerParams(
        dimension_semantics=("arbitrary",), vmem_limit_bytes=60 << 20, **more
    )


def shards(count, splits, latent, basis, event_bin, length, amplitude_scale, yield_norm, bin_coords):
    samples, waves, width = latent.shape
    total = bin_coords.shape[1]
    own = waves // count
    blocks = total // TILE
    tiles = blocks * (blocks + 1) // 2
    f32, bf16 = jnp.float32, jnp.bfloat16

    profile = jnp.stack(
        [length * length, amplitude_scale * jnp.sqrt(math.sqrt(2.0) * length)], axis=1
    ).reshape(count, own, 2, width)
    draws = jnp.transpose(latent, (1, 0, 2)).reshape(count, own, samples, width)

    batch = math.gcd(own, BATCHES)
    vmem = pl.BlockSpec(memory_space=pltpu.VMEM)
    piece = jax.ShapeDtypeStruct((count, own, samples, width), bf16)
    kern_spec = pl.BlockSpec((1, tiles, TILE, TILE), lambda w: (jnp.minimum(w, own - 1), 0, 0, 0))
    stages = [
        pltpu.VMEM((own, count, samples, width), bf16),
        pltpu.VMEM((count, own, samples, width), bf16),
    ]

    def semaphores(arrays):
        return [pltpu.SemaphoreType.DMA((arrays, batch, count - 1))] * 2 + [
            pltpu.SemaphoreType.DMA((own, count - 1))
        ] * 2

    kern, amp = pl.pallas_call(
        functools.partial(forward_kernel, "event", count, width, own, batch),
        out_shape=(jax.ShapeDtypeStruct((own, tiles, TILE, TILE), bf16), piece),
        grid=(own + 1,),
        in_specs=[vmem, vmem, vmem],
        out_specs=(kern_spec, vmem),
        scratch_shapes=[
            pltpu.VMEM((tiles, TILE, TILE), f32),
            pltpu.VMEM((total, LANES), f32),
            pltpu.VMEM((total, LANES), f32),
            pltpu.VMEM((blocks, 2, TILE), f32),
            pltpu.VMEM((blocks, samples, TILE), bf16),
            pltpu.VMEM((count, own, 2, width), f32),
            pltpu.VMEM((count, own, samples, width), bf16),
        ]
        + stages
        + semaphores(2),
        compiler_params=params(collective_id=0, has_side_effects=True),
        name="kern_forward",
    )(bin_coords, profile, draws)

    amp = amp.reshape(waves, samples, width)
    amp_rows = jnp.transpose(amp, (2, 1, 0)).reshape(width * samples, waves)
    amp_rows = jnp.pad(amp_rows, ((0, GROUP * samples), (0, 0)))

    events = basis.shape[0]
    block = min(events // splits, 4096)
    per = events // splits // block
    inner = block // CHUNK
    grouped = event_bin.reshape(events // CHUNK, CHUNK)
    first, last = grouped[:, 0], grouped[:, -1]
    basis_spec = pl.BlockSpec((block, waves), lambda e, *_: (e, 0))
    label_spec = pl.BlockSpec((1, block), lambda e, *_: (0, e))
    field_spec = pl.BlockSpec((1, samples, block), lambda e, *_: (e // per, 0, e % per))
    rows_spec = pl.BlockSpec(((width + GROUP) * samples, waves), lambda e, *_: (0, 0))
    field = pl.pallas_call(
        functools.partial(field_kernel, samples, inner),
        out_shape=jax.ShapeDtypeStruct((splits, samples, events // splits), bf16),
        grid_spec=pltpu.PrefetchScalarGridSpec(
            num_scalar_prefetch=2,
            grid=(events // block,),
            in_specs=[rows_spec, basis_spec, label_spec],
            out_specs=field_spec,
        ),
        compiler_params=params(),
        name="event_field",
    )(first, last, amp_rows, basis, event_bin)
    weight = share_weight("wave", splits, 2, samples, field)
    sums = pl.pallas_call(
        functools.partial(sums_kernel, samples, inner),
        out_shape=jax.ShapeDtypeStruct(((width + GROUP) * samples, waves), f32),
        grid_spec=pltpu.PrefetchScalarGridSpec(
            num_scalar_prefetch=2,
            grid=(events // block,),
            in_specs=[field_spec, basis_spec, label_spec],
            out_specs=rows_spec,
        ),
        compiler_params=params(),
        name="event_sums",
    )(first, last, weight, basis, event_bin)

    sums = jnp.transpose(sums[: width * samples].reshape(width, samples, waves), (2, 1, 0))
    grad = (sums + 2.0 / samples * amp.astype(f32) * yield_norm[:, None, :]).astype(bf16)
    pulled = pl.pallas_call(
        functools.partial(backward_kernel, "event", count, width, own, batch),
        out_shape=piece,
        grid=(own + 1,),
        in_specs=[kern_spec, vmem],
        out_specs=vmem,
        scratch_shapes=[
            pltpu.VMEM((blocks, samples, TILE), bf16),
            pltpu.VMEM((count, own, samples, width), bf16),
        ]
        + stages
        + semaphores(1),
        compiler_params=params(collective_id=1, has_side_effects=True),
        name="kern_backward",
    )(kern, grad.reshape(count, own, samples, width))
    pulled = pulled.reshape(waves, samples, width).astype(f32)
    return jnp.transpose(pulled, (1, 0, 2)) + latent.astype(f32)


def solution(mesh):
    placed = (
        P(None, "wave", "event"),
        P("event", "wave"),
        P("event", None),
        P("wave", "event"),
        P("wave", "event"),
        P("wave", "event"),
        P(),
    )
    return jax.shard_map(
        functools.partial(shards, mesh.shape["event"], mesh.shape["wave"]),
        mesh=mesh,
        in_specs=placed,
        out_specs=P(None, "wave", "event"),
        check_vma=False,
    )
```
